256 devices in a mesh: dp: 4 (over x), expert: 64 (over z, y, core).
Axes of the slice: x: 4, y: 4, z: 8, core: 2. Of those that a mesh axis runs over, the one named last changes fastest.
Arguments:
- tokens: bfloat16 [32768, 2048], P(('dp', 'expert')), may hold values from -6 to 6
- expert_ids: int32 [32768, 2], P(('dp', 'expert')), may hold values from 0 to 63, all different within a row; in each aligned block of 128 rows (0 to 127, 128 to 255, ...) at most 6 rows name the same one
- gates: bfloat16 [32768, 2], P(('dp', 'expert')), may hold values from 0.049804688 to 1
- cotangent: bfloat16 [32768, 2048], P(('dp', 'expert')), may hold values from -6 to 6
- w_gate: bfloat16 [64, 2048, 768], P('expert'), may hold values from -0.125 to 0.125
- w_up: bfloat16 [64, 2048, 768], P('expert'), may hold values from -0.125 to 0.125
- w_down: bfloat16 [64, 768, 2048], P('expert'), may hold values from -0.21875 to 0.21875
Outputs:
- grad_tokens: bfloat16 [32768, 2048], P(('dp', 'expert'))
- grad_gates: bfloat16 [32768, 2], P(('dp', 'expert'))
- grad_w_gate: bfloat16 [64, 2048, 768], P('expert', 'dp')
- grad_w_up: bfloat16 [64, 2048, 768], P('expert', 'dp')
- grad_w_down: bfloat16 [64, 768, 2048], P('expert', None, 'dp')
The draws below stay inside these ranges and needn't reach their ends.
Inputs may be any that keep to these rules, and one draw needn't show every extreme that they name: `expert_ids`: within the 128 rows of one device no expert is named by more than 6 rows, and in some of these aligned blocks an expert is named by exactly 6 rows.
All inputs are finite; a program needn't handle non-finite values.
Results may differ from the reference program's by a relative error of at most 0.013.
Values may be sent and summed in bfloat16 or wider, within the bound.
No kernel may reach another device: no remote copies, remote signals or barrier semaphores. Data moves between devices by JAX's collectives and lax.ppermute only.
A program may use at most 128 MiB of HBM per device.

```python
import math
import jax
import jax.numpy as jnp
import numpy as np
from jax import lax

D = 2048
FF = 768
TOK_DEV = 128
TOP = 2
EXPERTS = 64
CAP = 6
TOKENS = 32768
N_DP = 4
N_EXPERT = 64


def block_levels(key, shape, cuts, smallest, top_value):
    loudness = 1.0
    for axis_at, shards_of in cuts:
        draws = jax.random.uniform(jax.random.fold_in(jax.random.fold_in(key, 6), axis_at), (shards_of,), jnp.float32, smallest / len(cuts), top_value / len(cuts))
        loudness = loudness * jnp.repeat(jnp.exp(draws), shape[axis_at] // shards_of).reshape((-1,) + (1,) * (len(shape) - 1 - axis_at))
    return loudness


def shared_out(stream_key, own, number, rows, number_of, top, reach, slope):
    order = jax.random.permutation(stream_key, number_of)
    heavy_load, common = load_shares(number_of, rows * top, reach, slope, True), load_shares(number_of, rows * top, reach, slope, False)
    places = jnp.arange(number_of)

    def named(lengths, offset_by):
        used = int((lengths > 0).sum())
        fixed = max(1, used // 4)
        moved = fixed + (places - fixed + offset_by * (used - fixed)) % max(1, number_of - fixed)
        return jnp.zeros((number_of,), jnp.int32).at[order[jnp.where(places < fixed, places, moved)]].set(jnp.asarray(lengths, jnp.int32))

    lengths = jnp.where(number % 4 == 0, named(heavy_load, number // 4), named(common, number - number // 4 - 1))
    mixed = jax.random.permutation(jax.random.fold_in(own, 3), number_of)
    giver, receiver = mixed[0:number_of // 2 * 2:2], mixed[1:number_of // 2 * 2:2]
    room = jnp.minimum(lengths[giver] - 1, reach - lengths[receiver]) // 2
    room = jnp.where((giver == order[0]) | (receiver == order[0]) | (lengths[receiver] == 0), 0, jnp.maximum(room, 0))
    moved = jax.random.randint(jax.random.fold_in(own, 4), (number_of // 2,), 0, 1 << 20) % (room + 1)
    lengths = lengths.at[giver].add(-moved).at[receiver].add(moved)
    labels = jnp.searchsorted(jnp.cumsum(lengths), jnp.arange(rows * top), side="right").astype(jnp.int32)
    table = labels.reshape(top, rows).T
    table = table[jax.random.permutation(jax.random.fold_in(own, 1), rows)]
    offset_by = jax.random.randint(jax.random.fold_in(own, 2), (rows, 1), 0, top)
    return jnp.take_along_axis(table, (jnp.arange(top)[None, :] + offset_by) % top, axis=1)


def load_shares(count, total, limit, skew, full):
    portions = [(1 << 20) // math.isqrt(grade ** skew) + 1 for grade in range(1, count + 1)]
    largest = limit if full else min(limit, max(-(-total // count), total * portions[0] // sum(portions)))
    least = 1 if total - largest >= count - 1 else 0
    counts, rest = [largest] + [least] * (count - 1), total - largest - least * (count - 1)
    while rest > 0:
        free = [i for i in range(1, count) if counts[i] < largest] or [i for i in range(1, count) if counts[i] < limit]
        mass, remaining = sum([portions[i] for i in free]), rest
        for i in free:
            more = min(limit - counts[i], max(1, remaining * portions[i] // mass), rest)
            counts[i] = counts[i] + more
            rest = rest - more
    return np.array(counts)


def scatter_about(own_key, shape, spread, limit, shards=(), held_as=jnp.bfloat16):
    entries = spread * jax.random.normal(own_key, shape, jnp.float32)
    if shards:
        entries = entries * block_levels(own_key, shape, shards, -0.22, 0.18)
    return jnp.clip(entries, -limit, limit).astype(held_as)


def setup_inputs(seed: int = 0) -> dict:
    streams_of = jax.random.split(jax.random.key(seed), 8)
    tokens = scatter_about(streams_of[0], (TOKENS, D), 1.0, 6.0, ((0, 256),))
    expert_ids_keys = jax.random.split(jax.random.fold_in(streams_of[1], 1), TOKENS // TOK_DEV)
    expert_ids_turns = jax.random.permutation(jax.random.fold_in(streams_of[1], 3), TOKENS // TOK_DEV)
    expert_ids = jax.vmap(lambda own, number: shared_out(jax.random.fold_in(streams_of[1], 2), own, number, TOK_DEV, EXPERTS, TOP, CAP, 2))(expert_ids_keys, expert_ids_turns).reshape((TOKENS, TOP))
    gates = jnp.clip(jnp.exp(math.log(1.0) - 2.9996462 * jax.random.uniform(streams_of[2], (TOKENS, TOP), jnp.float32) ** block_levels(streams_of[2], (TOKENS, TOP), ((0, 256),), -0.2, 0.2)), 0.049804688, 1.0).astype(jnp.bfloat16)
    cotangent = scatter_about(streams_of[3], (TOKENS, D), 1.0, 6.0, ((0, 256),))
    w_gate = scatter_about(streams_of[4], (EXPERTS, D, FF), D ** -0.5, 0.125, ((0, 64),))
    w_up = scatter_about(streams_of[5], (EXPERTS, D, FF), D ** -0.5, 0.125, ((0, 64),))
    w_down = scatter_about(streams_of[6], (EXPERTS, FF, D), FF ** -0.5, 0.21875, ((0, 64),))
    return {"tokens": tokens, "expert_ids": expert_ids, "gates": gates, "cotangent": cotangent, "w_gate": w_gate, "w_up": w_up, "w_down": w_down}


def contract_rows(left, right):
    return lax.dot_general(left, right, (((0,), (0,)), ((), ())), preferred_element_type=jnp.float32)


def expert_pass(rows, cot_rows, gate_column, gate_mat, up_mat, down_mat):
    pre_gate = jnp.dot(rows, gate_mat, preferred_element_type=jnp.float32)
    pre_up = jnp.dot(rows, up_mat, preferred_element_type=jnp.float32)
    sigmoid_gate = jax.nn.sigmoid(pre_gate)
    activated = pre_gate * sigmoid_gate
    hidden = (activated * pre_up).astype(jnp.bfloat16)
    expert_out = jnp.dot(hidden, down_mat, preferred_element_type=jnp.float32)
    cot_float = cot_rows.astype(jnp.float32)
    score_grad = jnp.sum(expert_out * cot_float, axis=1)
    scaled = (gate_column.astype(jnp.float32)[:, None] * cot_float).astype(jnp.bfloat16)
    grad_hidden = jnp.dot(scaled, down_mat.T, preferred_element_type=jnp.float32)
    grad_pre_gate = (grad_hidden * pre_up * sigmoid_gate * (1.0 + pre_gate * (1.0 - sigmoid_gate))).astype(jnp.bfloat16)
    grad_pre_up = (grad_hidden * activated).astype(jnp.bfloat16)
    row_grad = (jnp.dot(grad_pre_gate, gate_mat.T, preferred_element_type=jnp.float32)
                + jnp.dot(grad_pre_up, up_mat.T, preferred_element_type=jnp.float32)).astype(jnp.bfloat16)
    return hidden, scaled, grad_pre_gate, grad_pre_up, row_grad, score_grad


def reference(tokens, expert_ids, gates, cotangent, w_gate, w_up, w_down):
    blocks = N_DP * N_EXPERT
    pair_count = TOK_DEV * TOP
    block_ids = expert_ids.reshape(blocks, pair_count)
    picked = (block_ids[:, :, None] == jnp.arange(EXPERTS, dtype=jnp.int32)[None, None, :]).astype(jnp.int32)
    before = jnp.cumsum(picked, axis=1) - picked
    position = jnp.sum(before * picked, axis=2).astype(jnp.int32)
    target = (block_ids * CAP + position).astype(jnp.int32)
    pair_global = jnp.arange(blocks * pair_count, dtype=jnp.int32).reshape(blocks, pair_count)
    block_index = jnp.arange(blocks, dtype=jnp.int32)[:, None]
    table = jnp.full((blocks, EXPERTS * CAP), -1, jnp.int32).at[block_index, target].set(pair_global)
    table = table.reshape(blocks, EXPERTS, CAP).transpose(1, 0, 2).reshape(EXPERTS, blocks * CAP)
    flat_gates = gates.reshape(-1)
    group_rows = N_EXPERT * CAP

    def group_total(left, right):
        total = jnp.zeros((left.shape[1], right.shape[1]), jnp.float32)
        for group in range(N_DP):
            part = contract_rows(left[group * group_rows:(group + 1) * group_rows],
                                 right[group * group_rows:(group + 1) * group_rows]).astype(jnp.bfloat16)
            total = total + lax.optimization_barrier(part).astype(jnp.float32)
        return total.astype(jnp.bfloat16)

    def one_expert(carry, inputs):
        grad_rows, score_acc = carry
        pair_index, gate_mat, up_mat, down_mat = inputs
        valid = pair_index >= 0
        safe_pair = jnp.where(valid, pair_index, 0).astype(jnp.int32)
        token_index = (safe_pair // TOP).astype(jnp.int32)
        rows = jnp.where(valid[:, None], tokens[token_index], jnp.zeros((), jnp.bfloat16))
        cot_rows = jnp.where(valid[:, None], cotangent[token_index], jnp.zeros((), jnp.bfloat16))
        gate_column = jnp.where(valid, flat_gates[safe_pair], jnp.zeros((), jnp.bfloat16))
        hidden, scaled, grad_pre_gate, grad_pre_up, row_grad, score_grad = expert_pass(
            rows, cot_rows, gate_column, gate_mat, up_mat, down_mat)
        grad_rows = grad_rows.at[token_index].add(jnp.where(valid[:, None], row_grad.astype(jnp.float32), jnp.zeros((), jnp.float32)))
        score_acc = score_acc.at[safe_pair].add(jnp.where(valid, score_grad, jnp.zeros((), jnp.float32)))
        grads = (group_total(rows, grad_pre_gate), group_total(rows, grad_pre_up), group_total(hidden, scaled))
        return (grad_rows, score_acc), grads

    start = (jnp.zeros((TOKENS, D), jnp.float32), jnp.zeros((TOKENS * TOP,), jnp.float32))
    (grad_rows, score_acc), (grad_w_gate, grad_w_up, grad_w_down) = lax.scan(
        one_expert, start, (table, w_gate, w_up, w_down))
    return (grad_rows.astype(jnp.bfloat16), score_acc.reshape(TOKENS, TOP).astype(jnp.bfloat16),
            grad_w_gate, grad_w_up, grad_w_down)
```

```python
import functools

import jax
import jax.numpy as jnp
import numpy as np
from jax import lax
from jax.experimental import pallas as pl
from jax.experimental.pallas import tpu as pltpu
from jax.sharding import PartitionSpec as P

BF = jnp.bfloat16
F32 = jnp.float32
PARTS = 4
HINT = 10
LINES = 8
GROUP = 8
LIMIT = 40 * 1024 * 1024
MOST = 60 * 1024 * 1024
SM = pl.BlockSpec(memory_space=pltpu.SMEM)


def dot(a, b):
    return jnp.dot(a, b, preferred_element_type=F32)


def dot_t(a, b):
    return lax.dot_general(a, b, (((1,), (1,)), ((), ())), preferred_element_type=F32)


def t_dot(a, b):
    return lax.dot_general(a, b, (((0,), (0,)), ((), ())), preferred_element_type=F32)


def whole(dims):
    return pl.BlockSpec(dims, lambda *_: (0,) * len(dims))


def call(kernel, outs, args, specs=None, out_specs=None, grid=(1,), scratch=(), flops=0, limit=LIMIT):
    size = sum(int(np.prod(a.shape)) * a.dtype.itemsize for a in list(args) + list(outs))
    return pl.pallas_call(
        kernel,
        out_shape=outs,
        grid=grid,
        in_specs=specs or [whole(a.shape) for a in args],
        out_specs=out_specs or [whole(a.shape) for a in outs],
        scratch_shapes=scratch,
        compiler_params=pltpu.CompilerParams(vmem_limit_bytes=limit),
        cost_estimate=pl.CostEstimate(flops=int(flops), bytes_accessed=size, transcendentals=0),
    )(*args)


def shape(dims, dtype=BF):
    return jax.ShapeDtypeStruct(dims, dtype)


def permutation(cap):
    rows = GROUP * PARTS * cap
    r = np.arange(rows)
    part, owner, slot = r // (GROUP * cap), r // cap % GROUP, r % cap
    mat = np.zeros((rows, rows), np.float32)
    mat[r, owner * PARTS * cap + part * cap + slot] = 1.0
    return mat


def line_permutation(cap):
    rows = GROUP * PARTS * cap
    r = np.arange(rows)
    block, owner, line = r // (GROUP * LINES), r // LINES % GROUP, r % LINES
    part, slot = (block * LINES + line) // cap, (block * LINES + line) % cap
    mat = np.zeros((rows, rows), np.float32)
    mat[r, part * GROUP * cap + owner * cap + slot] = 1.0
    return mat


def route(ids_ref, owners, cap):
    top, toks = ids_ref.shape
    experts = lax.broadcasted_iota(jnp.int32, (owners, toks), 0)
    earlier = jnp.where(
        lax.broadcasted_iota(jnp.int32, (toks, toks), 0) < lax.broadcasted_iota(jnp.int32, (toks, toks), 1), 1.0, 0.0
    ).astype(BF)
    seen = jnp.zeros((owners, 1), F32)
    picks, places, slots = [], [], []
    for k in range(top):
        ids = ids_ref[k : k + 1, :]
        pick = jnp.where(experts == ids, 1.0, 0.0)
        before = dot(pick.astype(BF), earlier) + seen
        seen = seen + jnp.sum(pick, axis=1, keepdims=True)
        place = jnp.sum(pick * before, axis=0, keepdims=True).astype(jnp.int32)
        picks.append(pick)
        places.append(place)
        slots.append(ids * cap + place)
    return picks, places, slots


def hits(slots, slot_count):
    rows = lax.broadcasted_iota(jnp.int32, (slot_count, slots[0].shape[1]), 0)
    return [rows == s for s in slots]


def pack(full_ref, packer_ref, out_ref, cap):
    block = GROUP * cap
    for g in range(full_ref.shape[0] // block):
        tall = tall_rows(full_ref, g, block)
        out_ref[g * block * PARTS : (g + 1) * block * PARTS, :] = t_dot(packer_ref[...], tall).astype(BF)


def unpack(in_ref, packer_ref, full_ref, cap):
    block, wide = GROUP * cap, in_ref.shape[1]
    for g in range(full_ref.shape[0] // block):
        tall = dot(packer_ref[...], in_ref[g * block * PARTS : (g + 1) * block * PARTS, :]).astype(BF)
        for q in range(PARTS):
            full_ref[g * block : (g + 1) * block, q * wide : (q + 1) * wide] = tall[q * block : (q + 1) * block, :]


def tall_rows(full_ref, g, block):
    wide = full_ref.shape[1] // PARTS
    return jnp.concatenate(
        [full_ref[g * block : (g + 1) * block, q * wide : (q + 1) * wide] for q in range(PARTS)], axis=0
    )


def pack_lines(full_ref, liner_ref, out_ref, cap):
    block, wide, high = GROUP * cap, full_ref.shape[1] // PARTS, GROUP * LINES
    for g in range(full_ref.shape[0] // block):
        lined = dot(liner_ref[...], tall_rows(full_ref, g, block)).astype(BF)
        for c in range(lined.shape[0] // high):
            out_ref[g * high : (g + 1) * high, c * wide : (c + 1) * wide] = lined[c * high : (c + 1) * high, :]


def unpack_lines(in_ref, liner_ref, full_ref, cap):
    block, wide, high = GROUP * cap, full_ref.shape[1] // PARTS, GROUP * LINES
    for g in range(full_ref.shape[0] // block):
        lined = jnp.concatenate(
            [in_ref[g * high : (g + 1) * high, c * wide : (c + 1) * wide] for c in range(PARTS * cap // LINES)], axis=0
        )
        tall = t_dot(liner_ref[...], lined).astype(BF)
        for q in range(PARTS):
            full_ref[g * block : (g + 1) * block, q * wide : (q + 1) * wide] = tall[q * block : (q + 1) * block, :]


def send_kernel(owners, cap, scaled, ids_ref, gates_ref, x_ref, packer_ref, out_ref, full_ref):
    _, _, slots = route(ids_ref, owners, cap)
    found = hits(slots, owners * cap)
    pick = jnp.where(functools.reduce(jnp.logical_or, found), 1.0, 0.0).astype(BF)
    full = dot(pick, x_ref[...])
    if scaled:
        weight = sum(
            jnp.where(f, gates_ref[k : k + 1, :].astype(F32), 0.0) for k, f in enumerate(found)
        )
        full = jnp.sum(weight, axis=1, keepdims=True) * full
    full_ref[...] = full.astype(BF)
    pack(full_ref, packer_ref, out_ref, cap)


def take_kernel(cap, pos_ref, in_ref, packer_ref, full_ref, own_ref, up_ref, down_ref):
    unpack(in_ref, packer_ref, full_ref, cap)
    wide = in_ref.shape[1]
    rows = full_ref.shape[0]
    half = rows // 2

    def quarter(j):
        return pl.ds(pl.multiple_of(lax.rem(pos_ref[0] + j, PARTS) * wide, wide), wide)

    own_ref[...] = full_ref[:, quarter(0)]
    up_ref[:rows, :] = full_ref[:, quarter(1)]
    up_ref[rows:, :] = full_ref[:half, quarter(2)]
    down_ref[:rows, :] = full_ref[:, quarter(3)]
    down_ref[rows:, :] = full_ref[half:, quarter(2)]


def forward_kernel(x_ref, wg_ref, wu_ref, pg_ref, pu_ref, h_ref):
    pre_gate = dot(x_ref[...], wg_ref[...])
    pre_up = dot(x_ref[...], wu_ref[...])
    pg_ref[...] = pre_gate
    pu_ref[...] = pre_up
    h_ref[...] = (pre_gate * jax.nn.sigmoid(pre_gate) * pre_up).astype(BF)


def backward_kernel(s_ref, wd_ref, pg_ref, pu_ref, g_ref, score_ref):
    n = pl.program_id(0)
    grad_hidden = dot_t(s_ref[...], wd_ref[...])
    pre_gate, pre_up = pg_ref[...], pu_ref[...]
    sig = jax.nn.sigmoid(pre_gate)
    act = pre_gate * sig
    hidden = (act * pre_up).astype(BF).astype(F32)
    g_ref[0] = (grad_hidden * pre_up * sig * (1.0 + pre_gate * (1.0 - sig))).astype(BF)
    g_ref[1] = (grad_hidden * act).astype(BF)
    part = jnp.sum(hidden * grad_hidden, axis=1, keepdims=True)

    @pl.when(n == 0)
    def _():
        score_ref[...] = part

    @pl.when(n > 0)
    def _():
        score_ref[...] += part


def back_kernel(cap, g_ref, wg_ref, wu_ref, score_ref, liner_ref, out_ref, full_ref):
    q = pl.program_id(0)
    wide = wg_ref.shape[0]
    cols = pl.ds(pl.multiple_of(q * wide, wide), wide)
    full_ref[:, cols] = (dot_t(g_ref[0], wg_ref[...]) + dot_t(g_ref[1], wu_ref[...])).astype(BF)

    @pl.when(q == pl.num_programs(0) - 1)
    def _():
        pack_lines(full_ref, liner_ref, out_ref, cap)
        slots = full_ref.shape[0]
        slot = lax.broadcasted_iota(jnp.int32, (slots, 128), 0).astype(F32)
        lane = lax.broadcasted_iota(jnp.int32, (slots, 128), 1).astype(F32)
        place = slot - cap * jnp.floor((slot + 0.5) * (1.0 / cap))
        spread = jnp.where(place == lane, score_ref[...], 0.0)
        owners = slots // cap
        first = lax.broadcasted_iota(jnp.int32, (owners, slots), 0) * cap
        col = lax.broadcasted_iota(jnp.int32, (owners, slots), 1)
        mine = jnp.where((col >= first) & (col < first + cap), 1.0, 0.0)
        found = jnp.dot(mine, spread, preferred_element_type=F32, precision=lax.Precision.HIGHEST).astype(BF)
        line = lax.broadcasted_iota(jnp.int32, (owners * LINES, owners), 0)
        owner = lax.broadcasted_iota(jnp.int32, (owners * LINES, owners), 1) * LINES
        out_ref[:, PARTS * cap // LINES * wide :] = dot(jnp.where(line == owner, 1.0, 0.0).astype(BF), found).astype(BF)


def finish_kernel(owners, cap, ids_ref, gates_ref, in_ref, liner_ref, gt_ref, gg_ref, full_ref):
    _, places, slots = route(ids_ref, owners, cap)
    unpack_lines(in_ref, liner_ref, full_ref, cap)
    pick = jnp.where(functools.reduce(jnp.logical_or, hits(slots, owners * cap)), 1.0, 0.0).astype(BF)
    gt_ref[...] = t_dot(pick, full_ref[...]).astype(BF)
    score = in_ref[:, in_ref.shape[1] - 128 :]
    lanes = lax.broadcasted_iota(jnp.int32, (128, ids_ref.shape[1]), 0)
    lines = lax.broadcasted_iota(jnp.int32, (owners * LINES, ids_ref.shape[1]), 0)
    for k, place in enumerate(places):
        chosen = jnp.where(lines == ids_ref[k : k + 1, :] * LINES, 1.0, 0.0).astype(BF)
        value = jnp.sum(jnp.where(lanes == place, t_dot(score, chosen), 0.0), axis=0, keepdims=True)
        gg_ref[k : k + 1, :] = (value / gates_ref[k : k + 1, :].astype(F32)).astype(BF)


def near_kernel(*refs):
    ins, outs = refs[:-3], refs[-3:]
    rows = ins[2].shape[0]
    gate = up = down = 0.0
    for i in range(0, len(ins), 4):
        x, s, h, g = ins[i : i + 4]
        gate = gate + t_dot(x[:rows, :], g[0])
        up = up + t_dot(x[:rows, :], g[1])
        down = down + t_dot(h[...], s[:rows, :])
    for out, total in zip(outs, (gate, up, down)):
        out[...] = total


def far_kernel(xa, xb, sa, sb, ha, hb, g0, g1, pgate, pup, pdown, gate, up, down):
    half = xa.shape[0]
    gate[...] = (pgate[...] + t_dot(xa[...], g0[:half, :]) + t_dot(xb[...], g0[half:, :])).astype(BF)
    up[...] = (pup[...] + t_dot(xa[...], g1[:half, :]) + t_dot(xb[...], g1[half:, :])).astype(BF)
    down[...] = (pdown[...] + t_dot(ha[...], sa[...]) + t_dot(hb[...], sb[...])).astype(BF)


def body(tokens, expert_ids, gates, cotangent, w_gate, w_up, w_down):
    toks, width = tokens.shape
    top = expert_ids.shape[1]
    owners = lax.axis_size("expert")
    groups = lax.axis_size("dp")
    cap = min(toks, 3 * toks * top // (2 * owners))
    slots = owners * cap
    half = slots // 2
    wg, wu, wd = w_gate[0], w_up[0], w_down[0]
    ff = wg.shape[1]
    wide = width // PARTS
    back_wide = PARTS * cap // LINES * wide + 128
    ids_t, gates_t = expert_ids.T, gates.T
    packer = jnp.asarray(permutation(cap), BF)
    liner = jnp.asarray(line_permutation(cap), BF)
    pos = lax.axis_index("dp").astype(jnp.int32).reshape(1)

    def go_up(v):
        return lax.ppermute(v, "dp", [(i, (i + 1) % groups) for i in range(groups)])

    def go_down(v):
        return lax.ppermute(v, "dp", [(i, (i - 1) % groups) for i in range(groups)])

    def exchange(v):
        v = v.reshape(owners, -1, v.shape[-1])
        v = lax.all_to_all(v, "expert", split_axis=0, concat_axis=0, tiled=True)
        return v.reshape(-1, v.shape[-1])

    def send(x, scaled):
        return call(
            functools.partial(send_kernel, owners, cap, scaled),
            [shape((slots * PARTS, wide))],
            [ids_t, gates_t, x, packer],
            scratch=[pltpu.VMEM((slots, width), BF)],
            flops=2 * slots * toks * width,
        )[0]

    def take(payload):
        return call(
            functools.partial(take_kernel, cap),
            [shape((slots, width)), shape((slots, wide)), shape((slots + half, wide)), shape((slots + half, wide))],
            [pos, payload, packer],
            specs=[SM, whole(payload.shape), whole(packer.shape)],
            flops=2 * slots * width * packer.shape[0],
        )

    by_col = lambda r: pl.BlockSpec((r, cut), lambda n: (0, n))
    cut = ff // 3

    sent_rows = exchange(send(tokens, False))
    sent_scaled = exchange(send(cotangent, True))

    rows, x_own, x_up, x_down = take(sent_rows)
    x_left, x_right = go_up(x_up), go_down(x_down)
    pre_gate, pre_up, hidden = call(
        forward_kernel,
        [shape((slots, ff), F32), shape((slots, ff), F32), shape((slots, ff))],
        [rows, wg, wu],
        specs=[whole((slots, width)), by_col(width), by_col(width)],
        out_specs=[by_col(slots), by_col(slots), by_col(slots)],
        grid=(3,),
        flops=4 * slots * width * ff,
    )
    hidden, x_left, x_right = lax.optimization_barrier((hidden, x_left, x_right))
    h_left, h_right = go_up(hidden), go_down(hidden)
    x_far = go_up(x_left[slots:]), go_down(x_right[slots:])
    h_left, h_right, x_far = lax.optimization_barrier((h_left, h_right, x_far))
    h_far = go_up(h_left[:half]), go_down(h_right[half:])
    sent_scaled, pre_gate, pre_up, h_far = lax.optimization_barrier((sent_scaled, pre_gate, pre_up, h_far))

    scaled, s_own, s_up, s_down = take(sent_scaled)
    s_left, s_right = go_up(s_up), go_down(s_down)
    grads, score = call(
        backward_kernel,
        [shape((2, slots, ff)), shape((slots, 1), F32)],
        [scaled, wd, pre_gate, pre_up],
        specs=[whole((slots, width)), pl.BlockSpec((cut, width), lambda n: (n, 0)), by_col(slots), by_col(slots)],
        out_specs=[pl.BlockSpec((2, slots, cut), lambda n: (0, 0, n)), whole((slots, 1))],
        grid=(3,),
        flops=2 * slots * width * ff,
    )
    g_left, g_right = go_up(grads), go_down(grads)
    by_row = pl.BlockSpec((wide, ff), lambda q: (q, 0))
    back = call(
        functools.partial(back_kernel, cap),
        [shape((owners * LINES, back_wide))],
        [grads, wg, wu, score, liner],
        specs=[whole(grads.shape), by_row, by_row, whole(score.shape), whole(liner.shape)],
        grid=(PARTS,),
        scratch=[pltpu.VMEM((slots, width), BF)],
        flops=4 * slots * width * ff,
    )[0]
    back_rows = exchange(back)
    s_far = go_up(s_left[slots:]), go_down(s_right[slots:])
    g_far = go_up(g_left[0]), go_down(g_right[1])
    grad_tokens, grad_gates_t = call(
        functools.partial(finish_kernel, owners, cap),
        [shape((toks, width)), shape((top, toks))],
        [ids_t, gates_t, back_rows, liner],
        scratch=[pltpu.VMEM((slots, width), BF)],
        flops=2 * slots * toks * width,
    )

    partial = call(
        near_kernel,
        [shape((wide, ff), F32), shape((wide, ff), F32), shape((ff, wide), F32)],
        [x_own, s_own, hidden, grads, x_left, s_left, h_left, g_left, x_right, s_right, h_right, g_right],
        flops=HINT * 6 * 3 * slots * wide * ff,
        limit=MOST,
    )
    grad_gate, grad_up, grad_down = call(
        far_kernel,
        [shape((wide, ff)), shape((wide, ff)), shape((ff, wide))],
        [*x_far, *s_far, *h_far, *g_far, *partial],
        flops=HINT * 6 * slots * wide * ff,
        limit=MOST,
    )
    return grad_tokens, grad_gates_t.T, grad_gate[None], grad_up[None], grad_down[None]


def solution(mesh):
    both = P(("dp", "expert"), None)
    held = P("expert", None, None)
    return jax.shard_map(
        body,
        mesh=mesh,
        in_specs=(both, both, both, both, held, held, held),
        out_specs=(both, both, P("expert", "dp", None), P("expert", "dp", None), P("expert", None, "dp")),
        check_vma=False,
    )
```

```python
import functools

import jax
import jax.numpy as jnp
import numpy as np
from jax import lax
from jax.experimental import pallas as pl
from jax.experimental.pallas import tpu as pltpu
from jax.sharding import PartitionSpec as P

BF = jnp.bfloat16
F32 = jnp.float32
PARTS = 4
HINT = 10
LINES = 8
GROUP = 8
LIMIT = 40 * 1024 * 1024
MOST = 60 * 1024 * 1024
SM = pl.BlockSpec(memory_space=pltpu.SMEM)


def dot(a, b):
    return jnp.dot(a, b, preferred_element_type=F32)


def dot_t(a, b):
    return lax.dot_general(a, b, (((1,), (1,)), ((), ())), preferred_element_type=F32)


def t_dot(a, b):
    return lax.dot_general(a, b, (((0,), (0,)), ((), ())), preferred_element_type=F32)


def whole(dims):
    return pl.BlockSpec(dims, lambda *_: (0,) * len(dims))


def call(kernel, outs, args, specs=None, out_specs=None, grid=(1,), scratch=(), flops=0, limit=LIMIT):
    size = sum(int(np.prod(a.shape)) * a.dtype.itemsize for a in list(args) + list(outs))
    return pl.pallas_call(
        kernel,
        out_shape=outs,
        grid=grid,
        in_specs=specs or [whole(a.shape) for a in args],
        out_specs=out_specs or [whole(a.shape) for a in outs],
        scratch_shapes=scratch,
        compiler_params=pltpu.CompilerParams(vmem_limit_bytes=limit),
        cost_estimate=pl.CostEstimate(flops=int(flops), bytes_accessed=size, transcendentals=0),
    )(*args)


def shape(dims, dtype=BF):
    return jax.ShapeDtypeStruct(dims, dtype)


def permutation(cap):
    rows = GROUP * PARTS * cap
    r = np.arange(rows)
    part, owner, slot = r // (GROUP * cap), r // cap % GROUP, r % cap
    mat = np.zeros((rows, rows), np.float32)
    mat[r, owner * PARTS * cap + part * cap + slot] = 1.0
    return mat


def line_permutation(cap):
    rows = GROUP * PARTS * cap
    r = np.arange(rows)
    block, owner, line = r // (GROUP * LINES), r // LINES % GROUP, r % LINES
    part, slot = (block * LINES + line) // cap, (block * LINES + line) % cap
    mat = np.zeros((rows, rows), np.float32)
    mat[r, part * GROUP * cap + owner * cap + slot] = 1.0
    return mat


def route(ids_ref, owners, cap):
    top, toks = ids_ref.shape
    experts = lax.broadcasted_iota(jnp.int32, (owners, toks), 0)
    earlier = jnp.where(
        lax.broadcasted_iota(jnp.int32, (toks, toks), 0) < lax.broadcasted_iota(jnp.int32, (toks, toks), 1), 1.0, 0.0
    ).astype(BF)
    seen = jnp.zeros((owners, 1), F32)
    picks, places, slots = [], [], []
    for k in range(top):
        ids = ids_ref[k : k + 1, :]
        pick = jnp.where(experts == ids, 1.0, 0.0)
        before = dot(pick.astype(BF), earlier) + seen
        seen = seen + jnp.sum(pick, axis=1, keepdims=True)
        place = jnp.sum(pick * before, axis=0, keepdims=True).astype(jnp.int32)
        picks.append(pick)
        places.append(place)
        slots.append(ids * cap + place)
    return picks, places, slots


def hits(slots, slot_count):
    rows = lax.broadcasted_iota(jnp.int32, (slot_count, slots[0].shape[1]), 0)
    return [rows == s for s in slots]


def pack(full_ref, packer_ref, out_ref, cap):
    block = GROUP * cap
    for g in range(full_ref.shape[0] // block):
        tall = tall_rows(full_ref, g, block)
        out_ref[g * block * PARTS : (g + 1) * block * PARTS, :] = t_dot(packer_ref[...], tall).astype(BF)


def unpack(in_ref, packer_ref, full_ref, cap):
    block, wide = GROUP * cap, in_ref.shape[1]
    for g in range(full_ref.shape[0] // block):
        tall = dot(packer_ref[...], in_ref[g * block * PARTS : (g + 1) * block * PARTS, :]).astype(BF)
        for q in range(PARTS):
            full_ref[g * block : (g + 1) * block, q * wide : (q + 1) * wide] = tall[q * block : (q + 1) * block, :]


def tall_rows(full_ref, g, block):
    wide = full_ref.shape[1] // PARTS
    return jnp.concatenate(
        [full_ref[g * block : (g + 1) * block, q * wide : (q + 1) * wide] for q in range(PARTS)], axis=0
    )


def pack_lines(full_ref, liner_ref, out_ref, cap):
    block, wide, high = GROUP * cap, full_ref.shape[1] // PARTS, GROUP * LINES
    for g in range(full_ref.shape[0] // block):
        lined = dot(liner_ref[...], tall_rows(full_ref, g, block)).astype(BF)
        for c in range(lined.shape[0] // high):
            out_ref[g * high : (g + 1) * high, c * wide : (c + 1) * wide] = lined[c * high : (c + 1) * high, :]


def unpack_lines(in_ref, liner_ref, full_ref, cap):
    block, wide, high = GROUP * cap, full_ref.shape[1] // PARTS, GROUP * LINES
    for g in range(full_ref.shape[0] // block):
        lined = jnp.concatenate(
            [in_ref[g * high : (g + 1) * high, c * wide : (c + 1) * wide] for c in range(PARTS * cap // LINES)], axis=0
        )
        tall = t_dot(liner_ref[...], lined).astype(BF)
        for q in range(PARTS):
            full_ref[g * block : (g + 1) * block, q * wide : (q + 1) * wide] = tall[q * block : (q + 1) * block, :]


def send_kernel(owners, cap, scaled, ids_ref, gates_ref, x_ref, packer_ref, out_ref, full_ref):
    _, _, slots = route(ids_ref, owners, cap)
    found = hits(slots, owners * cap)
    pick = jnp.where(functools.reduce(jnp.logical_or, found), 1.0, 0.0).astype(BF)
    full = dot(pick, x_ref[...])
    if scaled:
        weight = sum(
            jnp.where(f, gates_ref[k : k + 1, :].astype(F32), 0.0) for k, f in enumerate(found)
        )
        full = jnp.sum(weight, axis=1, keepdims=True) * full
    full_ref[...] = full.astype(BF)
    pack(full_ref, packer_ref, out_ref, cap)


def take_kernel(cap, pos_ref, in_ref, packer_ref, full_ref, *piece_refs):
    unpack(in_ref, packer_ref, full_ref, cap)
    wide = in_ref.shape[1]
    for j, piece in enumerate(piece_refs):
        at = pl.multiple_of(lax.rem(pos_ref[0] + j, PARTS) * wide, wide)
        piece[...] = full_ref[:, pl.ds(at, wide)]


def forward_kernel(x_ref, wg_ref, wu_ref, pg_ref, pu_ref, h_ref):
    pre_gate = dot(x_ref[...], wg_ref[...])
    pre_up = dot(x_ref[...], wu_ref[...])
    pg_ref[...] = pre_gate
    pu_ref[...] = pre_up
    h_ref[...] = (pre_gate * jax.nn.sigmoid(pre_gate) * pre_up).astype(BF)


def backward_kernel(cap, pos_ref, in_ref, packer_ref, wd_ref, pg_ref, pu_ref, g_ref, score_ref, *rest):
    *piece_refs, full_ref = rest
    n = pl.program_id(0)

    @pl.when(n == 0)
    def _():
        take_kernel(cap, pos_ref, in_ref, packer_ref, full_ref, *piece_refs)

    grad_hidden = dot_t(full_ref[...], wd_ref[...])
    pre_gate, pre_up = pg_ref[...], pu_ref[...]
    sig = jax.nn.sigmoid(pre_gate)
    act = pre_gate * sig
    hidden = (act * pre_up).astype(BF).astype(F32)
    g_ref[0] = (grad_hidden * pre_up * sig * (1.0 + pre_gate * (1.0 - sig))).astype(BF)
    g_ref[1] = (grad_hidden * act).astype(BF)
    part = jnp.sum(hidden * grad_hidden, axis=1, keepdims=True)

    @pl.when(n == 0)
    def _():
        score_ref[...] = part

    @pl.when(n > 0)
    def _():
        score_ref[...] += part


def back_kernel(cap, g_ref, wg_ref, wu_ref, score_ref, liner_ref, out_ref, full_ref):
    q = pl.program_id(0)
    wide = wg_ref.shape[0]
    cols = pl.ds(pl.multiple_of(q * wide, wide), wide)
    full_ref[:, cols] = (dot_t(g_ref[0], wg_ref[...]) + dot_t(g_ref[1], wu_ref[...])).astype(BF)

    @pl.when(q == pl.num_programs(0) - 1)
    def _():
        pack_lines(full_ref, liner_ref, out_ref, cap)
        slots = full_ref.shape[0]
        slot = lax.broadcasted_iota(jnp.int32, (slots, 128), 0).astype(F32)
        lane = lax.broadcasted_iota(jnp.int32, (slots, 128), 1).astype(F32)
        place = slot - cap * jnp.floor((slot + 0.5) * (1.0 / cap))
        spread = jnp.where(place == lane, score_ref[...], 0.0)
        owners = slots // cap
        first = lax.broadcasted_iota(jnp.int32, (owners, slots), 0) * cap
        col = lax.broadcasted_iota(jnp.int32, (owners, slots), 1)
        mine = jnp.where((col >= first) & (col < first + cap), 1.0, 0.0)
        found = jnp.dot(mine, spread, preferred_element_type=F32, precision=lax.Precision.HIGHEST).astype(BF)
        line = lax.broadcasted_iota(jnp.int32, (owners * LINES, owners), 0)
        owner = lax.broadcasted_iota(jnp.int32, (owners * LINES, owners), 1) * LINES
        out_ref[:, PARTS * cap // LINES * wide :] = dot(jnp.where(line == owner, 1.0, 0.0).astype(BF), found).astype(BF)


def finish_kernel(owners, cap, ids_ref, gates_ref, in_ref, liner_ref, gt_ref, gg_ref, full_ref):
    _, places, slots = route(ids_ref, owners, cap)
    unpack_lines(in_ref, liner_ref, full_ref, cap)
    pick = jnp.where(functools.reduce(jnp.logical_or, hits(slots, owners * cap)), 1.0, 0.0).astype(BF)
    gt_ref[...] = t_dot(pick, full_ref[...]).astype(BF)
    score = in_ref[:, in_ref.shape[1] - 128 :]
    lanes = lax.broadcasted_iota(jnp.int32, (128, ids_ref.shape[1]), 0)
    lines = lax.broadcasted_iota(jnp.int32, (owners * LINES, ids_ref.shape[1]), 0)
    for k, place in enumerate(places):
        chosen = jnp.where(lines == ids_ref[k : k + 1, :] * LINES, 1.0, 0.0).astype(BF)
        value = jnp.sum(jnp.where(lanes == place, t_dot(score, chosen), 0.0), axis=0, keepdims=True)
        gg_ref[k : k + 1, :] = (value / gates_ref[k : k + 1, :].astype(F32)).astype(BF)


def near_kernel(*refs):
    ins, outs = refs[:-2], refs[-2:]
    for k, out in enumerate(outs):
        out[...] = sum(t_dot(x[...], g[k]) for x, g in zip(ins[::2], ins[1::2]))


def last_kernel(x, g0, g1, pgate, pup, *refs):
    near, (ha, hb, s), (gate, up, down) = refs[:-6], refs[-6:-3], refs[-3:]
    half = ha.shape[0]
    gate[...] = (pgate[...] + t_dot(x[...], g0[...])).astype(BF)
    up[...] = (pup[...] + t_dot(x[...], g1[...])).astype(BF)
    far = t_dot(ha[...], s[:half, :]) + t_dot(hb[...], s[half:, :])
    down[...] = (sum(t_dot(h[...], v[...]) for h, v in zip(near[::2], near[1::2])) + far).astype(BF)


def body(tokens, expert_ids, gates, cotangent, w_gate, w_up, w_down):
    toks, width = tokens.shape
    top = expert_ids.shape[1]
    owners = lax.axis_size("expert")
    groups = lax.axis_size("dp")
    cap = min(toks, 3 * toks * top // (2 * owners))
    slots = owners * cap
    half = slots // 2
    wg, wu, wd = w_gate[0], w_up[0], w_down[0]
    ff = wg.shape[1]
    wide = width // PARTS
    back_wide = PARTS * cap // LINES * wide + 128
    ids_t, gates_t = expert_ids.T, gates.T
    packer = jnp.asarray(permutation(cap), BF)
    liner = jnp.asarray(line_permutation(cap), BF)
    pos = lax.axis_index("dp").astype(jnp.int32).reshape(1)

    def go_up(v):
        return lax.ppermute(v, "dp", [(i, (i + 1) % groups) for i in range(groups)])

    def go_across(v):
        return lax.ppermute(v, "dp", [(i, (i + 2) % groups) for i in range(groups)])

    def go_down(v):
        return lax.ppermute(v, "dp", [(i, (i - 1) % groups) for i in range(groups)])

    def exchange(v):
        v = v.reshape(owners, -1, v.shape[-1])
        v = lax.all_to_all(v, "expert", split_axis=0, concat_axis=0, tiled=True)
        return v.reshape(-1, v.shape[-1])

    def send(x, scaled):
        return call(
            functools.partial(send_kernel, owners, cap, scaled),
            [shape((slots * PARTS, wide))],
            [ids_t, gates_t, x, packer],
            scratch=[pltpu.VMEM((slots, width), BF)],
            flops=2 * slots * toks * width,
            limit=MOST,
        )[0]

    def take(payload):
        return call(
            functools.partial(take_kernel, cap),
            [shape((slots, width))] + [shape((slots, wide))] * PARTS,
            [pos, payload, packer],
            specs=[SM, whole(payload.shape), whole(packer.shape)],
            flops=2 * slots * width * packer.shape[0],
        )

    by_col = lambda r: pl.BlockSpec((r, cut), lambda n: (0, n))
    cut = ff // 3

    sent_rows = exchange(send(tokens, False))
    sent_scaled = exchange(send(cotangent, True))

    rows, x_own, x_next, x_across, x_last = take(sent_rows)
    x_left, x_right, x_far = go_up(x_next), go_down(x_last), go_across(x_across)
    pre_gate, pre_up, hidden = call(
        forward_kernel,
        [shape((slots, ff), F32), shape((slots, ff), F32), shape((slots, ff))],
        [rows, wg, wu],
        specs=[whole((slots, width)), by_col(width), by_col(width)],
        out_specs=[by_col(slots), by_col(slots), by_col(slots)],
        grid=(3,),
        flops=4 * slots * width * ff,
        limit=MOST,
    )
    hidden, x_left, x_right = lax.optimization_barrier((hidden, x_left, x_right))
    h_left, h_right = go_up(hidden), go_down(hidden)
    sent_scaled, x_far, h_left, h_right = lax.optimization_barrier((sent_scaled, x_far, h_left, h_right))
    h_far = go_up(h_left[:half]), go_down(h_right[half:])

    grads, score, s_own, s_next, s_across, s_last = call(
        functools.partial(backward_kernel, cap),
        [shape((2, slots, ff)), shape((slots, 1), F32)] + [shape((slots, wide))] * PARTS,
        [pos, sent_scaled, packer, wd, pre_gate, pre_up],
        specs=[SM, whole(sent_scaled.shape), whole(packer.shape), pl.BlockSpec((cut, width), lambda n: (n, 0)), by_col(slots), by_col(slots)],
        out_specs=[pl.BlockSpec((2, slots, cut), lambda n: (0, 0, n)), whole((slots, 1))] + [whole((slots, wide))] * PARTS,
        grid=(3,),
        scratch=[pltpu.VMEM((slots, width), BF)],
        flops=2 * slots * width * ff,
        limit=MOST,
    )
    grads, score, h_far = lax.optimization_barrier((grads, score, h_far))
    g_left, g_right = go_up(grads), go_down(grads)
    by_row = pl.BlockSpec((wide, ff), lambda q: (q, 0))
    back = call(
        functools.partial(back_kernel, cap),
        [shape((owners * LINES, back_wide))],
        [grads, wg, wu, score, liner],
        specs=[whole(grads.shape), by_row, by_row, whole(score.shape), whole(liner.shape)],
        grid=(PARTS,),
        scratch=[pltpu.VMEM((slots, width), BF)],
        flops=4 * slots * width * ff,
        limit=MOST,
    )[0]
    back_rows = exchange(back)
    g_left, g_right, s_next, s_across, s_last = lax.optimization_barrier((g_left, g_right, s_next, s_across, s_last))
    g_far = go_up(g_left[0]), go_down(g_right[1])
    s_left, s_right, s_far = go_up(s_next), go_down(s_last), go_across(s_across)
    grad_tokens, grad_gates_t = call(
        functools.partial(finish_kernel, owners, cap),
        [shape((toks, width)), shape((top, toks))],
        [ids_t, gates_t, back_rows, liner],
        scratch=[pltpu.VMEM((slots, width), BF)],
        flops=2 * slots * toks * width,
    )

    partial = call(
        near_kernel,
        [shape((wide, ff), F32), shape((wide, ff), F32)],
        [x_own, grads, x_left, g_left, x_right, g_right],
        flops=HINT * 4 * 3 * slots * wide * ff,
        limit=MOST,
    )
    grad_gate, grad_up, grad_down = call(
        last_kernel,
        [shape((wide, ff)), shape((wide, ff)), shape((ff, wide))],
        [x_far, *g_far, *partial, hidden, s_own, h_left, s_left, h_right, s_right, *h_far, s_far],
        flops=HINT * 12 * slots * wide * ff,
        limit=MOST,
    )
    return grad_tokens, grad_gates_t.T, grad_gate[None], grad_up[None], grad_down[None]


def solution(mesh):
    both = P(("dp", "expert"), None)
    held = P("expert", None, None)
    return jax.shard_map(
        body,
        mesh=mesh,
        in_specs=(both, both, both, both, held, held, held),
        out_specs=(both, both, P("expert", "dp", None), P("expert", "dp", None), P("expert", None, "dp")),
        check_vma=False,
    )
```

```python
import functools

import jax
import jax.numpy as jnp
import numpy as np
from jax import lax
from jax.experimental import pallas as pl
from jax.experimental.pallas import tpu as pltpu
from jax.sharding import PartitionSpec as P

BF = jnp.bfloat16
F32 = jnp.float32
PARTS = 4
HINT = 10
LINES = 8
GROUP = 8
LIMIT = 40 * 1024 * 1024
MOST = 60 * 1024 * 1024
SM = pl.BlockSpec(memory_space=pltpu.SMEM)


def dot(a, b):
    return jnp.dot(a, b, preferred_element_type=F32)


def dot_t(a, b):
    return lax.dot_general(a, b, (((1,), (1,)), ((), ())), preferred_element_type=F32)


def t_dot(a, b):
    return lax.dot_general(a, b, (((0,), (0,)), ((), ())), preferred_element_type=F32)


def whole(dims):
    return pl.BlockSpec(dims, lambda *_: (0,) * len(dims))


def call(kernel, outs, args, specs=None, out_specs=None, grid=(1,), scratch=(), flops=0, limit=LIMIT):
    size = sum(int(np.prod(a.shape)) * a.dtype.itemsize for a in list(args) + list(outs))
    return pl.pallas_call(
        kernel,
        out_shape=outs,
        grid=grid,
        in_specs=specs or [whole(a.shape) for a in args],
        out_specs=out_specs or [whole(a.shape) for a in outs],
        scratch_shapes=scratch,
        compiler_params=pltpu.CompilerParams(vmem_limit_bytes=limit),
        cost_estimate=pl.CostEstimate(flops=int(flops), bytes_accessed=size, transcendentals=0),
    )(*args)


def shape(dims, dtype=BF):
    return jax.ShapeDtypeStruct(dims, dtype)


def permutation(cap):
    rows = GROUP * PARTS * cap
    r = np.arange(rows)
    part, owner, slot = r // (GROUP * cap), r // cap % GROUP, r % cap
    mat = np.zeros((rows, rows), np.float32)
    mat[r, owner * PARTS * cap + part * cap + slot] = 1.0
    return mat


def line_permutation(cap):
    rows = GROUP * PARTS * cap
    r = np.arange(rows)
    block, owner, line = r // (GROUP * LINES), r // LINES % GROUP, r % LINES
    part, slot = (block * LINES + line) // cap, (block * LINES + line) % cap
    mat = np.zeros((rows, rows), np.float32)
    mat[r, part * GROUP * cap + owner * cap + slot] = 1.0
    return mat


def route(ids_ref, owners, cap):
    top, toks = ids_ref.shape
    experts = lax.broadcasted_iota(jnp.int32, (owners, toks), 0)
    earlier = jnp.where(
        lax.broadcasted_iota(jnp.int32, (toks, toks), 0) < lax.broadcasted_iota(jnp.int32, (toks, toks), 1), 1.0, 0.0
    ).astype(BF)
    seen = jnp.zeros((owners, 1), F32)
    picks, places, slots = [], [], []
    for k in range(top):
        ids = ids_ref[k : k + 1, :]
        pick = jnp.where(experts == ids, 1.0, 0.0)
        before = dot(pick.astype(BF), earlier) + seen
        seen = seen + jnp.sum(pick, axis=1, keepdims=True)
        place = jnp.sum(pick * before, axis=0, keepdims=True).astype(jnp.int32)
        picks.append(pick)
        places.append(place)
        slots.append(ids * cap + place)
    return picks, places, slots


def hits(slots, slot_count):
    rows = lax.broadcasted_iota(jnp.int32, (slot_count, slots[0].shape[1]), 0)
    return [rows == s for s in slots]


def pack(full_ref, packer_ref, out_ref, cap):
    block = GROUP * cap
    for g in range(full_ref.shape[0] // block):
        tall = tall_rows(full_ref, g, block)
        out_ref[g * block * PARTS : (g + 1) * block * PARTS, :] = t_dot(packer_ref[...], tall).astype(BF)


def unpack(in_ref, packer_ref, full_ref, cap):
    block, wide = GROUP * cap, in_ref.shape[1]
    for g in range(full_ref.shape[0] // block):
        tall = dot(packer_ref[...], in_ref[g * block * PARTS : (g + 1) * block * PARTS, :]).astype(BF)
        for q in range(PARTS):
            full_ref[g * block : (g + 1) * block, q * wide : (q + 1) * wide] = tall[q * block : (q + 1) * block, :]


def tall_rows(full_ref, g, block):
    wide = full_ref.shape[1] // PARTS
    return jnp.concatenate(
        [full_ref[g * block : (g + 1) * block, q * wide : (q + 1) * wide] for q in range(PARTS)], axis=0
    )


def pack_lines(full_ref, liner_ref, out_ref, cap):
    block, wide, high = GROUP * cap, full_ref.shape[1] // PARTS, GROUP * LINES
    for g in range(full_ref.shape[0] // block):
        lined = dot(liner_ref[...], tall_rows(full_ref, g, block)).astype(BF)
        for c in range(lined.shape[0] // high):
            out_ref[g * high : (g + 1) * high, c * wide : (c + 1) * wide] = lined[c * high : (c + 1) * high, :]


def unpack_lines(in_ref, liner_ref, full_ref, cap):
    block, wide, high = GROUP * cap, full_ref.shape[1] // PARTS, GROUP * LINES
    for g in range(full_ref.shape[0] // block):
        lined = jnp.concatenate(
            [in_ref[g * high : (g + 1) * high, c * wide : (c + 1) * wide] for c in range(PARTS * cap // LINES)], axis=0
        )
        tall = t_dot(liner_ref[...], lined).astype(BF)
        for q in range(PARTS):
            full_ref[g * block : (g + 1) * block, q * wide : (q + 1) * wide] = tall[q * block : (q + 1) * block, :]


def send_kernel(owners, cap, scaled, ids_ref, gates_ref, x_ref, packer_ref, out_ref, full_ref):
    _, _, slots = route(ids_ref, owners, cap)
    found = hits(slots, owners * cap)
    pick = jnp.where(functools.reduce(jnp.logical_or, found), 1.0, 0.0).astype(BF)
    full = dot(pick, x_ref[...])
    if scaled:
        weight = sum(
            jnp.where(f, gates_ref[k : k + 1, :].astype(F32), 0.0) for k, f in enumerate(found)
        )
        full = jnp.sum(weight, axis=1, keepdims=True) * full
    full_ref[...] = full.astype(BF)
    pack(full_ref, packer_ref, out_ref, cap)


def take_kernel(cap, pos_ref, in_ref, packer_ref, full_ref, *piece_refs):
    unpack(in_ref, packer_ref, full_ref, cap)
    wide = in_ref.shape[1]
    for j, piece in enumerate(piece_refs):
        at = pl.multiple_of(lax.rem(pos_ref[0] + j, PARTS) * wide, wide)
        piece[...] = full_ref[:, pl.ds(at, wide)]


def forward_kernel(x_ref, wg_ref, wu_ref, pg_ref, pu_ref, h_ref):
    pre_gate = dot(x_ref[...], wg_ref[...])
    pre_up = dot(x_ref[...], wu_ref[...])
    pg_ref[...] = pre_gate
    pu_ref[...] = pre_up
    h_ref[...] = (pre_gate * jax.nn.sigmoid(pre_gate) * pre_up).astype(BF)


def backward_kernel(cap, pos_ref, in_ref, packer_ref, wd_ref, pg_ref, pu_ref, g_ref, score_ref, *rest):
    *piece_refs, full_ref = rest
    n = pl.program_id(0)

    @pl.when(n == 0)
    def _():
        take_kernel(cap, pos_ref, in_ref, packer_ref, full_ref, *piece_refs)

    grad_hidden = dot_t(full_ref[...], wd_ref[...])
    pre_gate, pre_up = pg_ref[...], pu_ref[...]
    sig = jax.nn.sigmoid(pre_gate)
    act = pre_gate * sig
    hidden = (act * pre_up).astype(BF).astype(F32)
    g_ref[0] = (grad_hidden * pre_up * sig * (1.0 + pre_gate * (1.0 - sig))).astype(BF)
    g_ref[1] = (grad_hidden * act).astype(BF)
    part = jnp.sum(hidden * grad_hidden, axis=1, keepdims=True)

    @pl.when(n == 0)
    def _():
        score_ref[...] = part

    @pl.when(n > 0)
    def _():
        score_ref[...] += part


def back_kernel(cap, g_ref, wg_ref, wu_ref, score_ref, liner_ref, out_ref, full_ref):
    q = pl.program_id(0)
    wide = wg_ref.shape[0]
    cols = pl.ds(pl.multiple_of(q * wide, wide), wide)
    full_ref[:, cols] = (dot_t(g_ref[0], wg_ref[...]) + dot_t(g_ref[1], wu_ref[...])).astype(BF)

    @pl.when(q == pl.num_programs(0) - 1)
    def _():
        pack_lines(full_ref, liner_ref, out_ref, cap)
        slots = full_ref.shape[0]
        slot = lax.broadcasted_iota(jnp.int32, (slots, 128), 0).astype(F32)
        lane = lax.broadcasted_iota(jnp.int32, (slots, 128), 1).astype(F32)
        place = slot - cap * jnp.floor((slot + 0.5) * (1.0 / cap))
        spread = jnp.where(place == lane, score_ref[...], 0.0)
        owners = slots // cap
        first = lax.broadcasted_iota(jnp.int32, (owners, slots), 0) * cap
        col = lax.broadcasted_iota(jnp.int32, (owners, slots), 1)
        mine = jnp.where((col >= first) & (col < first + cap), 1.0, 0.0)
        found = jnp.dot(mine, spread, preferred_element_type=F32, precision=lax.Precision.HIGHEST).astype(BF)
        line = lax.broadcasted_iota(jnp.int32, (owners * LINES, owners), 0)
        owner = lax.broadcasted_iota(jnp.int32, (owners * LINES, owners), 1) * LINES
        out_ref[:, PARTS * cap // LINES * wide :] = dot(jnp.where(line == owner, 1.0, 0.0).astype(BF), found).astype(BF)


def finish_kernel(owners, cap, ids_ref, gates_ref, in_ref, liner_ref, gt_ref, gg_ref, full_ref):
    _, places, slots = route(ids_ref, owners, cap)
    unpack_lines(in_ref, liner_ref, full_ref, cap)
    pick = jnp.where(functools.reduce(jnp.logical_or, hits(slots, owners * cap)), 1.0, 0.0).astype(BF)
    gt_ref[...] = t_dot(pick, full_ref[...]).astype(BF)
    score = in_ref[:, in_ref.shape[1] - 128 :]
    lanes = lax.broadcasted_iota(jnp.int32, (128, ids_ref.shape[1]), 0)
    lines = lax.broadcasted_iota(jnp.int32, (owners * LINES, ids_ref.shape[1]), 0)
    for k, place in enumerate(places):
        chosen = jnp.where(lines == ids_ref[k : k + 1, :] * LINES, 1.0, 0.0).astype(BF)
        value = jnp.sum(jnp.where(lanes == place, t_dot(score, chosen), 0.0), axis=0, keepdims=True)
        gg_ref[k : k + 1, :] = (value / gates_ref[k : k + 1, :].astype(F32)).astype(BF)


def near_kernel(far_ref, *refs):
    ins, (gate, up, turned) = refs[:-3], refs[-3:]
    turned[...] = far_ref[...].T
    for k, out in enumerate((gate, up)):
        out[...] = sum(t_dot(x[...], g[k]) for x, g in zip(ins[::2], ins[1::2]))


def down_kernel(*refs):
    near, (ha, hb, s, down) = refs[:-4], refs[-4:]
    half = ha.shape[0]
    far = t_dot(ha[...], s[:half, :]) + t_dot(hb[...], s[half:, :])
    down[...] = (sum(t_dot(h[...], v[...]) for h, v in zip(near[::2], near[1::2])) + far).astype(BF)


def last_kernel(x, g0, g1, pgate, pup, gate, up):
    gate[...] = (pgate[...] + dot(x[...], g0[...])).astype(BF)
    up[...] = (pup[...] + dot(x[...], g1[...])).astype(BF)


def body(tokens, expert_ids, gates, cotangent, w_gate, w_up, w_down):
    toks, width = tokens.shape
    top = expert_ids.shape[1]
    owners = lax.axis_size("expert")
    groups = lax.axis_size("dp")
    cap = min(toks, 3 * toks * top // (2 * owners))
    slots = owners * cap
    half = slots // 2
    wg, wu, wd = w_gate[0], w_up[0], w_down[0]
    ff = wg.shape[1]
    wide = width // PARTS
    back_wide = PARTS * cap // LINES * wide + 128
    ids_t, gates_t = expert_ids.T, gates.T
    packer = jnp.asarray(permutation(cap), BF)
    liner = jnp.asarray(line_permutation(cap), BF)
    pos = lax.axis_index("dp").astype(jnp.int32).reshape(1)

    def go_up(v):
        return lax.ppermute(v, "dp", [(i, (i + 1) % groups) for i in range(groups)])

    def go_across(v):
        return lax.ppermute(v, "dp", [(i, (i + 2) % groups) for i in range(groups)])

    def go_down(v):
        return lax.ppermute(v, "dp", [(i, (i - 1) % groups) for i in range(groups)])

    def exchange(v):
        v = v.reshape(owners, -1, v.shape[-1])
        v = lax.all_to_all(v, "expert", split_axis=0, concat_axis=0, tiled=True)
        return v.reshape(-1, v.shape[-1])

    def send(x, scaled):
        return call(
            functools.partial(send_kernel, owners, cap, scaled),
            [shape((slots * PARTS, wide))],
            [ids_t, gates_t, x, packer],
            scratch=[pltpu.VMEM((slots, width), BF)],
            flops=2 * slots * toks * width,
            limit=MOST,
        )[0]

    def take(payload):
        return call(
            functools.partial(take_kernel, cap),
            [shape((slots, width))] + [shape((slots, wide))] * PARTS,
            [pos, payload, packer],
            specs=[SM, whole(payload.shape), whole(packer.shape)],
            flops=2 * slots * width * packer.shape[0],
        )

    by_col = lambda r: pl.BlockSpec((r, cut), lambda n: (0, n))
    cut = ff // 3

    sent_rows = exchange(send(tokens, False))
    sent_scaled = exchange(send(cotangent, True))

    rows, x_own, x_next, x_across, x_last = take(sent_rows)
    x_left, x_right, x_far = go_up(x_next), go_down(x_last), go_across(x_across)
    pre_gate, pre_up, hidden = call(
        forward_kernel,
        [shape((slots, ff), F32), shape((slots, ff), F32), shape((slots, ff))],
        [rows, wg, wu],
        specs=[whole((slots, width)), by_col(width), by_col(width)],
        out_specs=[by_col(slots), by_col(slots), by_col(slots)],
        grid=(3,),
        flops=4 * slots * width * ff,
        limit=MOST,
    )
    hidden, x_left, x_right = lax.optimization_barrier((hidden, x_left, x_right))
    h_left, h_right = go_up(hidden), go_down(hidden)
    sent_scaled, x_far, h_left, h_right = lax.optimization_barrier((sent_scaled, x_far, h_left, h_right))
    h_far = go_up(h_left[:half]), go_down(h_right[half:])

    grads, score, s_own, s_next, s_across, s_last = call(
        functools.partial(backward_kernel, cap),
        [shape((2, slots, ff)), shape((slots, 1), F32)] + [shape((slots, wide))] * PARTS,
        [pos, sent_scaled, packer, wd, pre_gate, pre_up],
        specs=[SM, whole(sent_scaled.shape), whole(packer.shape), pl.BlockSpec((cut, width), lambda n: (n, 0)), by_col(slots), by_col(slots)],
        out_specs=[pl.BlockSpec((2, slots, cut), lambda n: (0, 0, n)), whole((slots, 1))] + [whole((slots, wide))] * PARTS,
        grid=(3,),
        scratch=[pltpu.VMEM((slots, width), BF)],
        flops=2 * slots * width * ff,
        limit=MOST,
    )
    grads, score, h_far = lax.optimization_barrier((grads, score, h_far))
    g_left, g_right = go_up(grads), go_down(grads)
    by_row = pl.BlockSpec((wide, ff), lambda q: (q, 0))
    back = call(
        functools.partial(back_kernel, cap),
        [shape((owners * LINES, back_wide))],
        [grads, wg, wu, score, liner],
        specs=[whole(grads.shape), by_row, by_row, whole(score.shape), whole(liner.shape)],
        grid=(PARTS,),
        scratch=[pltpu.VMEM((slots, width), BF)],
        flops=4 * slots * width * ff,
        limit=MOST,
    )[0]
    back_rows = exchange(back)
    g_left, g_right, s_next, s_across, s_last = lax.optimization_barrier((g_left, g_right, s_next, s_across, s_last))
    s_left, s_right, s_far = go_up(s_next), go_down(s_last), go_across(s_across)
    g_first, g_second, s_left, s_right, s_far = lax.optimization_barrier(
        (g_left[0], g_right[1], s_left, s_right, s_far)
    )
    g_first, g_second = go_up(g_first), go_down(g_second)
    grad_tokens, grad_gates_t = call(
        functools.partial(finish_kernel, owners, cap),
        [shape((toks, width)), shape((top, toks))],
        [ids_t, gates_t, back_rows, liner],
        scratch=[pltpu.VMEM((slots, width), BF)],
        flops=2 * slots * toks * width,
    )

    *partial, x_turned = call(
        near_kernel,
        [shape((wide, ff), F32), shape((wide, ff), F32), shape((wide, slots))],
        [x_far, x_own, grads, x_left, g_left, x_right, g_right],
        flops=HINT * 4 * 3 * slots * wide * ff,
        limit=MOST,
    )
    grad_down = call(
        down_kernel,
        [shape((ff, wide))],
        [hidden, s_own, h_left, s_left, h_right, s_right, *h_far, s_far],
        flops=HINT * 8 * slots * wide * ff,
        limit=MOST,
    )[0]
    grad_gate, grad_up = call(
        last_kernel,
        [shape((wide, ff)), shape((wide, ff))],
        [x_turned, g_first, g_second, *partial],
        specs=[whole(x_turned.shape), by_col(slots), by_col(slots), by_col(wide), by_col(wide)],
        out_specs=[by_col(wide), by_col(wide)],
        grid=(3,),
        flops=HINT * 4 * slots * wide * ff,
        limit=MOST,
    )
    return grad_tokens, grad_gates_t.T, grad_gate[None], grad_up[None], grad_down[None]


def solution(mesh):
    both = P(("dp", "expert"), None)
    held = P("expert", None, None)
    return jax.shard_map(
        body,
        mesh=mesh,
        in_specs=(both, both, both, both, held, held, held),
        out_specs=(both, both, P("expert", "dp", None), P("expert", "dp", None), P("expert", None, "dp")),
        check_vma=False,
    )
```

```python
import functools

import jax
import jax.numpy as jnp
import numpy as np
from jax import lax
from jax.experimental import pallas as pl
from jax.experimental.pallas import tpu as pltpu
from jax.sharding import PartitionSpec as P

BF = jnp.bfloat16
F32 = jnp.float32
PARTS = 4
HINT = 10
LINES = 8
GROUP = 8
LIMIT = 40 * 1024 * 1024
MOST = 60 * 1024 * 1024
SMALL = 24 * 1024 * 1024
SM = pl.BlockSpec(memory_space=pltpu.SMEM)


def dot(a, b):
    return jnp.dot(a, b, preferred_element_type=F32)


def dot_t(a, b):
    return lax.dot_general(a, b, (((1,), (1,)), ((), ())), preferred_element_type=F32)


def t_dot(a, b):
    return lax.dot_general(a, b, (((0,), (0,)), ((), ())), preferred_element_type=F32)


def whole(dims):
    return pl.BlockSpec(dims, lambda *_: (0,) * len(dims))


def call(kernel, outs, args, specs=None, out_specs=None, grid=(1,), scratch=(), flops=0, limit=LIMIT):
    size = sum(int(np.prod(a.shape)) * a.dtype.itemsize for a in list(args) + list(outs))
    return pl.pallas_call(
        kernel,
        out_shape=outs,
        grid=grid,
        in_specs=specs or [whole(a.shape) for a in args],
        out_specs=out_specs or [whole(a.shape) for a in outs],
        scratch_shapes=scratch,
        compiler_params=pltpu.CompilerParams(vmem_limit_bytes=limit),
        cost_estimate=pl.CostEstimate(flops=int(flops), bytes_accessed=size, transcendentals=0),
    )(*args)


def shape(dims, dtype=BF):
    return jax.ShapeDtypeStruct(dims, dtype)


def permutation(cap):
    rows = GROUP * PARTS * cap
    r = np.arange(rows)
    part, owner, slot = r // (GROUP * cap), r // cap % GROUP, r % cap
    mat = np.zeros((rows, rows), np.float32)
    mat[r, owner * PARTS * cap + part * cap + slot] = 1.0
    return mat


def line_permutation(cap):
    rows = GROUP * PARTS * cap
    r = np.arange(rows)
    block, owner, line = r // (GROUP * LINES), r // LINES % GROUP, r % LINES
    part, slot = (block * LINES + line) // cap, (block * LINES + line) % cap
    mat = np.zeros((rows, rows), np.float32)
    mat[r, part * GROUP * cap + owner * cap + slot] = 1.0
    return mat


def route(ids_ref, owners, cap):
    top, toks = ids_ref.shape
    experts = lax.broadcasted_iota(jnp.int32, (owners, toks), 0)
    earlier = jnp.where(
        lax.broadcasted_iota(jnp.int32, (toks, toks), 0) < lax.broadcasted_iota(jnp.int32, (toks, toks), 1), 1.0, 0.0
    ).astype(BF)
    seen = jnp.zeros((owners, 1), F32)
    picks, places, slots = [], [], []
    for k in range(top):
        ids = ids_ref[k : k + 1, :]
        pick = jnp.where(experts == ids, 1.0, 0.0)
        before = dot(pick.astype(BF), earlier) + seen
        seen = seen + jnp.sum(pick, axis=1, keepdims=True)
        place = jnp.sum(pick * before, axis=0, keepdims=True).astype(jnp.int32)
        picks.append(pick)
        places.append(place)
        slots.append(ids * cap + place)
    return picks, places, slots


def hits(slots, slot_count):
    rows = lax.broadcasted_iota(jnp.int32, (slot_count, slots[0].shape[1]), 0)
    return [rows == s for s in slots]


def pack(full_ref, packer_ref, out_ref, cap):
    block = GROUP * cap
    for g in range(full_ref.shape[0] // block):
        tall = tall_rows(full_ref, g, block)
        out_ref[g * block * PARTS : (g + 1) * block * PARTS, :] = t_dot(packer_ref[...], tall).astype(BF)


def unpack(in_ref, packer_ref, full_ref, cap):
    block, wide = GROUP * cap, in_ref.shape[1]
    for g in range(full_ref.shape[0] // block):
        tall = dot(packer_ref[...], in_ref[g * block * PARTS : (g + 1) * block * PARTS, :]).astype(BF)
        for q in range(PARTS):
            full_ref[g * block : (g + 1) * block, q * wide : (q + 1) * wide] = tall[q * block : (q + 1) * block, :]


def tall_rows(full_ref, g, block):
    wide = full_ref.shape[1] // PARTS
    return jnp.concatenate(
        [full_ref[g * block : (g + 1) * block, q * wide : (q + 1) * wide] for q in range(PARTS)], axis=0
    )


def pack_lines(full_ref, liner_ref, out_ref, cap):
    block, wide, high = GROUP * cap, full_ref.shape[1] // PARTS, GROUP * LINES
    for g in range(full_ref.shape[0] // block):
        lined = dot(liner_ref[...], tall_rows(full_ref, g, block)).astype(BF)
        for c in range(lined.shape[0] // high):
            out_ref[g * high : (g + 1) * high, c * wide : (c + 1) * wide] = lined[c * high : (c + 1) * high, :]


def unpack_lines(in_ref, liner_ref, full_ref, cap):
    block, wide, high = GROUP * cap, full_ref.shape[1] // PARTS, GROUP * LINES
    for g in range(full_ref.shape[0] // block):
        lined = jnp.concatenate(
            [in_ref[g * high : (g + 1) * high, c * wide : (c + 1) * wide] for c in range(PARTS * cap // LINES)], axis=0
        )
        tall = t_dot(liner_ref[...], lined).astype(BF)
        for q in range(PARTS):
            full_ref[g * block : (g + 1) * block, q * wide : (q + 1) * wide] = tall[q * block : (q + 1) * block, :]


def send_kernel(owners, cap, scaled, ids_ref, gates_ref, x_ref, packer_ref, out_ref, full_ref):
    _, _, slots = route(ids_ref, owners, cap)
    found = hits(slots, owners * cap)
    pick = jnp.where(functools.reduce(jnp.logical_or, found), 1.0, 0.0).astype(BF)
    full = dot(pick, x_ref[...])
    if scaled:
        weight = sum(
            jnp.where(f, gates_ref[k : k + 1, :].astype(F32), 0.0) for k, f in enumerate(found)
        )
        full = jnp.sum(weight, axis=1, keepdims=True) * full
    full_ref[...] = full.astype(BF)
    pack(full_ref, packer_ref, out_ref, cap)


def take_kernel(cap, pos_ref, in_ref, packer_ref, full_ref, *piece_refs):
    unpack(in_ref, packer_ref, full_ref, cap)
    wide = in_ref.shape[1]
    for j, piece in enumerate(piece_refs):
        at = pl.multiple_of(lax.rem(pos_ref[0] + j, PARTS) * wide, wide)
        piece[...] = full_ref[:, pl.ds(at, wide)]


def forward_kernel(x_ref, wg_ref, wu_ref, pg_ref, pu_ref, h_ref):
    pre_gate = dot(x_ref[...], wg_ref[...])
    pre_up = dot(x_ref[...], wu_ref[...])
    pg_ref[...] = pre_gate
    pu_ref[...] = pre_up
    h_ref[...] = (pre_gate * jax.nn.sigmoid(pre_gate) * pre_up).astype(BF)


def backward_kernel(cap, pos_ref, in_ref, packer_ref, wd_ref, pg_ref, pu_ref, g_ref, score_ref, *rest):
    *piece_refs, full_ref = rest
    n = pl.program_id(0)

    @pl.when(n == 0)
    def _():
        take_kernel(cap, pos_ref, in_ref, packer_ref, full_ref, *piece_refs)

    grad_hidden = dot_t(full_ref[...], wd_ref[...])
    pre_gate, pre_up = pg_ref[...], pu_ref[...]
    sig = jax.nn.sigmoid(pre_gate)
    act = pre_gate * sig
    hidden = (act * pre_up).astype(BF).astype(F32)
    g_ref[0] = (grad_hidden * pre_up * sig * (1.0 + pre_gate * (1.0 - sig))).astype(BF)
    g_ref[1] = (grad_hidden * act).astype(BF)
    part = jnp.sum(hidden * grad_hidden, axis=1, keepdims=True)

    @pl.when(n == 0)
    def _():
        score_ref[...] = part

    @pl.when(n > 0)
    def _():
        score_ref[...] += part


def back_kernel(cap, g_ref, wg_ref, wu_ref, score_ref, liner_ref, out_ref, full_ref):
    q = pl.program_id(0)
    wide = wg_ref.shape[0]
    cols = pl.ds(pl.multiple_of(q * wide, wide), wide)
    full_ref[:, cols] = (dot_t(g_ref[0], wg_ref[...]) + dot_t(g_ref[1], wu_ref[...])).astype(BF)

    @pl.when(q == pl.num_programs(0) - 1)
    def _():
        pack_lines(full_ref, liner_ref, out_ref, cap)
        slots = full_ref.shape[0]
        slot = lax.broadcasted_iota(jnp.int32, (slots, 128), 0).astype(F32)
        lane = lax.broadcasted_iota(jnp.int32, (slots, 128), 1).astype(F32)
        place = slot - cap * jnp.floor((slot + 0.5) * (1.0 / cap))
        spread = jnp.where(place == lane, score_ref[...], 0.0)
        owners = slots // cap
        first = lax.broadcasted_iota(jnp.int32, (owners, slots), 0) * cap
        col = lax.broadcasted_iota(jnp.int32, (owners, slots), 1)
        mine = jnp.where((col >= first) & (col < first + cap), 1.0, 0.0)
        found = jnp.dot(mine, spread, preferred_element_type=F32, precision=lax.Precision.HIGHEST).astype(BF)
        line = lax.broadcasted_iota(jnp.int32, (owners * LINES, owners), 0)
        owner = lax.broadcasted_iota(jnp.int32, (owners * LINES, owners), 1) * LINES
        out_ref[:, PARTS * cap // LINES * wide :] = dot(jnp.where(line == owner, 1.0, 0.0).astype(BF), found).astype(BF)


def finish_kernel(owners, cap, ids_ref, gates_ref, in_ref, liner_ref, gt_ref, gg_ref, full_ref):
    _, places, slots = route(ids_ref, owners, cap)
    unpack_lines(in_ref, liner_ref, full_ref, cap)
    pick = jnp.where(functools.reduce(jnp.logical_or, hits(slots, owners * cap)), 1.0, 0.0).astype(BF)
    gt_ref[...] = t_dot(pick, full_ref[...]).astype(BF)
    score = in_ref[:, in_ref.shape[1] - 128 :]
    lanes = lax.broadcasted_iota(jnp.int32, (128, ids_ref.shape[1]), 0)
    lines = lax.broadcasted_iota(jnp.int32, (owners * LINES, ids_ref.shape[1]), 0)
    for k, place in enumerate(places):
        chosen = jnp.where(lines == ids_ref[k : k + 1, :] * LINES, 1.0, 0.0).astype(BF)
        value = jnp.sum(jnp.where(lanes == place, t_dot(score, chosen), 0.0), axis=0, keepdims=True)
        gg_ref[k : k + 1, :] = (value / gates_ref[k : k + 1, :].astype(F32)).astype(BF)


def near_kernel(far_ref, *refs):
    ins, (gate, up, turned) = refs[:-3], refs[-3:]
    turned[...] = far_ref[...].T
    for k, out in enumerate((gate, up)):
        out[...] = sum(t_dot(x[...], g[k]) for x, g in zip(ins[::2], ins[1::2]))


def down_kernel(*refs):
    near, (ha, hb, s, down) = refs[:-4], refs[-4:]
    half = ha.shape[0]
    far = t_dot(ha[...], s[:half, :]) + t_dot(hb[...], s[half:, :])
    down[...] = (sum(t_dot(h[...], v[...]) for h, v in zip(near[::2], near[1::2])) + far).astype(BF)


def last_kernel(x, g0, g1, pgate, pup, gate, up):
    gate[...] = (pgate[...] + dot(x[...], g0[...])).astype(BF)
    up[...] = (pup[...] + dot(x[...], g1[...])).astype(BF)


def body(tokens, expert_ids, gates, cotangent, w_gate, w_up, w_down):
    toks, width = tokens.shape
    top = expert_ids.shape[1]
    owners = lax.axis_size("expert")
    groups = lax.axis_size("dp")
    cap = min(toks, 3 * toks * top // (2 * owners))
    slots = owners * cap
    half = slots // 2
    wg, wu, wd = w_gate[0], w_up[0], w_down[0]
    ff = wg.shape[1]
    wide = width // PARTS
    back_wide = PARTS * cap // LINES * wide + 128
    ids_t, gates_t = expert_ids.T, gates.T
    packer = jnp.asarray(permutation(cap), BF)
    liner = jnp.asarray(line_permutation(cap), BF)
    pos = lax.axis_index("dp").astype(jnp.int32).reshape(1)

    def go_up(v):
        return lax.ppermute(v, "dp", [(i, (i + 1) % groups) for i in range(groups)])

    def go_across(v):
        return lax.ppermute(v, "dp", [(i, (i + 2) % groups) for i in range(groups)])

    def go_down(v):
        return lax.ppermute(v, "dp", [(i, (i - 1) % groups) for i in range(groups)])

    def exchange(v):
        v = v.reshape(owners, -1, v.shape[-1])
        v = lax.all_to_all(v, "expert", split_axis=0, concat_axis=0, tiled=True)
        return v.reshape(-1, v.shape[-1])

    def send(x, scaled):
        return call(
            functools.partial(send_kernel, owners, cap, scaled),
            [shape((slots * PARTS, wide))],
            [ids_t, gates_t, x, packer],
            scratch=[pltpu.VMEM((slots, width), BF)],
            flops=2 * slots * toks * width,
            limit=MOST,
        )[0]

    def take(payload):
        return call(
            functools.partial(take_kernel, cap),
            [shape((slots, width))] + [shape((slots, wide))] * PARTS,
            [pos, payload, packer],
            specs=[SM, whole(payload.shape), whole(packer.shape)],
            flops=2 * slots * width * packer.shape[0],
        )

    by_col = lambda r: pl.BlockSpec((r, cut), lambda n: (0, n))
    cut = ff // 3

    sent_rows = exchange(send(tokens, False))
    sent_scaled = exchange(send(cotangent, True))

    rows, x_own, x_next, x_across, x_last = take(sent_rows)
    x_left, x_right, x_far = go_up(x_next), go_down(x_last), go_across(x_across)
    pre_gate, pre_up, hidden = call(
        forward_kernel,
        [shape((slots, ff), F32), shape((slots, ff), F32), shape((slots, ff))],
        [rows, wg, wu],
        specs=[whole((slots, width)), by_col(width), by_col(width)],
        out_specs=[by_col(slots), by_col(slots), by_col(slots)],
        grid=(3,),
        flops=4 * slots * width * ff,
        limit=MOST,
    )
    hidden, x_left, x_right = lax.optimization_barrier((hidden, x_left, x_right))
    h_left, h_right = go_up(hidden), go_down(hidden)
    sent_scaled, x_far, h_left, h_right = lax.optimization_barrier((sent_scaled, x_far, h_left, h_right))
    h_far = go_up(h_left[:half]), go_down(h_right[half:])

    grads, score, s_own, s_next, s_across, s_last = call(
        functools.partial(backward_kernel, cap),
        [shape((2, slots, ff)), shape((slots, 1), F32)] + [shape((slots, wide))] * PARTS,
        [pos, sent_scaled, packer, wd, pre_gate, pre_up],
        specs=[SM, whole(sent_scaled.shape), whole(packer.shape), pl.BlockSpec((cut, width), lambda n: (n, 0)), by_col(slots), by_col(slots)],
        out_specs=[pl.BlockSpec((2, slots, cut), lambda n: (0, 0, n)), whole((slots, 1))] + [whole((slots, wide))] * PARTS,
        grid=(3,),
        scratch=[pltpu.VMEM((slots, width), BF)],
        flops=2 * slots * width * ff,
        limit=MOST,
    )
    grads, score, h_far = lax.optimization_barrier((grads, score, h_far))
    g_left, g_right = go_up(grads), go_down(grads)
    by_row = pl.BlockSpec((wide, ff), lambda q: (q, 0))
    back = call(
        functools.partial(back_kernel, cap),
        [shape((owners * LINES, back_wide))],
        [grads, wg, wu, score, liner],
        specs=[whole(grads.shape), by_row, by_row, whole(score.shape), whole(liner.shape)],
        grid=(PARTS,),
        scratch=[pltpu.VMEM((slots, width), BF)],
        flops=4 * slots * width * ff,
        limit=MOST,
    )[0]
    back_rows = exchange(back)
    g_left, g_right, s_next, s_across, s_last = lax.optimization_barrier((g_left, g_right, s_next, s_across, s_last))
    s_left, s_right, s_far = go_up(s_next), go_down(s_last), go_across(s_across)
    g_first, g_second, s_left, s_right, s_far = lax.optimization_barrier(
        (g_left[0], g_right[1], s_left, s_right, s_far)
    )
    g_first, g_second = go_up(g_first), go_down(g_second)
    grad_tokens, grad_gates_t = call(
        functools.partial(finish_kernel, owners, cap),
        [shape((toks, width)), shape((top, toks))],
        [ids_t, gates_t, back_rows, liner],
        scratch=[pltpu.VMEM((slots, width), BF)],
        flops=2 * slots * toks * width,
    )

    *partial, x_turned = call(
        near_kernel,
        [shape((wide, ff), F32), shape((wide, ff), F32), shape((wide, slots))],
        [x_far, x_own, grads, x_left, g_left, x_right, g_right],
        flops=HINT * 4 * 3 * slots * wide * ff,
        limit=SMALL,
    )
    grad_down = call(
        down_kernel,
        [shape((ff, wide))],
        [hidden, s_own, h_left, s_left, h_right, s_right, *h_far, s_far],
        flops=HINT * 8 * slots * wide * ff,
        limit=SMALL,
    )[0]
    grad_gate, grad_up = call(
        last_kernel,
        [shape((wide, ff)), shape((wide, ff))],
        [x_turned, g_first, g_second, *partial],
        specs=[whole(x_turned.shape), by_col(slots), by_col(slots), by_col(wide), by_col(wide)],
        out_specs=[by_col(wide), by_col(wide)],
        grid=(3,),
        flops=HINT * 4 * slots * wide * ff,
        limit=SMALL,
    )
    return grad_tokens, grad_gates_t.T, grad_gate[None], grad_up[None], grad_down[None]


def solution(mesh):
    both = P(("dp", "expert"), None)
    held = P("expert", None, None)
    return jax.shard_map(
        body,
        mesh=mesh,
        in_specs=(both, both, both, both, held, held, held),
        out_specs=(both, both, P("expert", "dp", None), P("expert", "dp", None), P("expert", None, "dp")),
        check_vma=False,
    )
```
